32 devices in a mesh: pipe: 2 (over x), section: 4 (over y, core), tensor: 4 (over z).
Axes of the slice: x: 2, y: 2, z: 4, core: 2. Of those that a mesh axis runs over, the one named last changes fastest.
Arguments:
- section_input: bfloat16 [2, 4, 384, 2560], P('pipe', 'section', None, 'tensor'), may hold values from -120 to 120
- section_cotan: bfloat16 [2, 4, 384, 2560], P('pipe', 'section', None, 'tensor'), may hold values from -6 to 6
- weights: bfloat16 [6, 2560, 2560], P(None, 'pipe', 'tensor'), may hold values from -0.125 to 0.125
- section_cuts: int32 [3, 5], replicated, may hold values from 0 to 6, as said below
- pipe_template: int32 [2], replicated, may hold values from 0 to 2
Outputs:
- weight_grads: float32 [6, 2560, 2560], P(None, ('pipe', 'section'), 'tensor')
The draws below stay inside these ranges and needn't reach their ends.
Inputs may be any that keep to these rules, and one draw needn't show every extreme that they name: `section_cuts`: row t starts at 0 and ends with 6; each section holds 1 or 2 layers, and 2 sections of every template hold 2.
All inputs are finite; a program needn't handle non-finite values.
Results may differ from the reference program's by a relative error of at most 0.0039.
Values may be sent and summed in bfloat16 or wider, within the bound.
A program may use at most 128 MiB of HBM per device.

```python
import math
import jax
import jax.numpy as jnp
from jax import lax

D = 2560
LAYERS = 6
TEMPLATES = 3
TOK = 384
PIPES = 2
SECTIONS = 4


def draw_section_input(key, part):
    subkeys = jax.random.split(key, 3)
    full_shape = (PIPES, SECTIONS, TOK, D)
    columns = jnp.exp(jax.random.uniform(subkeys[1], (D,), jnp.float32, 0.0, math.log(10.0)))
    row_scale = jnp.exp(jax.random.uniform(subkeys[2], (PIPES, SECTIONS, TOK, 1), jnp.float32, 0.0, math.log(3.0)))
    draws_base = jnp.clip(jax.random.normal(subkeys[0], full_shape, jnp.float32), -4.0, 4.0)
    return (draws_base * columns * row_scale).astype(jnp.bfloat16)


def draw_section_cuts(key, part):
    surplus = LAYERS - SECTIONS

    def single_template(template_index):
        ranking = jax.random.permutation(jax.random.fold_in(key, template_index), SECTIONS)
        section_sizes = 1 + (ranking < surplus).astype(jnp.int32)
        return jnp.concatenate([jnp.zeros((1,), jnp.int32), jnp.cumsum(section_sizes).astype(jnp.int32)])
    return jnp.stack([single_template(template_index) for template_index in range(TEMPLATES)])


def levels(stream_key, dims, shards, least, top_value):
    def one(dim, shards_of):
        heights = jax.random.uniform(jax.random.fold_in(jax.random.fold_in(stream_key, 6), dim), (shards_of,), jnp.float32, least / len(shards), top_value / len(shards))
        return jnp.repeat(jnp.exp(heights), dims[dim] // shards_of).reshape((-1,) + (1,) * (len(dims) - dim - 1))

    factor_of = one(*shards[0])
    for cut in shards[1:]:
        factor_of = factor_of * one(*cut)
    return factor_of


def noise(key, shape, spread, bound, cuts=(), kind=jnp.bfloat16):
    drawn = jax.random.normal(key, shape, jnp.float32) * spread
    if len(cuts) > 0:
        drawn = levels(key, shape, cuts, -0.22, 0.18) * drawn
    return jnp.clip(drawn, min=-bound, max=bound).astype(kind)


def setup_inputs(seed: int = 0) -> dict:
    splits = jax.random.split(jax.random.key(seed), 6)
    return {
        "section_input": draw_section_input(jax.random.fold_in(splits[5], 71), 0),
        "section_cotan": noise(splits[1], (PIPES, SECTIONS, TOK, D), 1.0, 6.0, ((0, 2), (1, 4), (3, 4))),
        "weights": noise(splits[2], (LAYERS, D, D), D ** -0.5, 0.125, ((1, 2), (2, 4))),
        "section_cuts": draw_section_cuts(jax.random.fold_in(splits[5], 71), 0),
        "pipe_template": jax.random.randint(splits[4], (PIPES,), 0, TEMPLATES).astype(jnp.int32),
    }


epsilon = 1e-05

def forward_rows(values):
    inv_rms = lax.rsqrt(lax.optimization_barrier(jnp.mean(values * values, axis=1, keepdims=True)) + epsilon)
    active = jax.nn.silu(values * inv_rms).astype(jnp.bfloat16)
    return (inv_rms, active)

def reference(section_input, section_cotan, weights, section_cuts, pipe_template):
    layers = weights.shape[0]

    def one_pipe(totals, pipe_items):
        inputs, cotans, template = pipe_items
        template_pick = (jnp.arange(TEMPLATES, dtype=jnp.int32) == template).astype(jnp.int32)
        bounds = lax.optimization_barrier(jnp.sum(template_pick[:, None] * section_cuts, axis=0)).astype(jnp.int32)
        for section_index in range(SECTIONS):
            first = bounds[section_index]
            section_stop = bounds[section_index + 1]
            second = jnp.minimum(first + 1, layers - 1).astype(jnp.int32)
            second_live = (first + 1 < section_stop).astype(jnp.float32)
            first_matrix = lax.dynamic_index_in_dim(weights, first, 0, keepdims=False)
            second_matrix = lax.dynamic_index_in_dim(weights, second, 0, keepdims=False)
            h_first = inputs[section_index].astype(jnp.float32)
            inv_first, active_first = forward_rows(h_first)
            raised = h_first + jnp.dot(active_first, first_matrix, preferred_element_type=jnp.float32)
            h_second = lax.optimization_barrier(raised.astype(jnp.bfloat16)).astype(jnp.float32)
            inv_second, active_second = forward_rows(h_second)
            cotan = cotans[section_index].astype(jnp.float32)
            cotan_low = cotans[section_index]
            grad_second = jnp.dot(active_second.T, cotan_low, preferred_element_type=jnp.float32) * second_live
            summed = jnp.dot(cotan_low, second_matrix.T, preferred_element_type=jnp.float32)
            normed = h_second * inv_second
            gate_sig = jax.nn.sigmoid(normed)
            d_norm = summed * gate_sig * (1.0 + normed * (1.0 - gate_sig))
            mean_term = lax.optimization_barrier(jnp.mean(h_second * d_norm, axis=1, keepdims=True))
            d_rows = inv_second * d_norm - h_second * inv_second * inv_second * inv_second * mean_term
            cotan_first = cotan + second_live * d_rows
            grad_first = jnp.dot(active_first.T, cotan_first.astype(jnp.bfloat16), preferred_element_type=jnp.float32)
            totals = totals.at[first].add(grad_first)
            totals = totals.at[second].add(grad_second)
        return (totals, None)
    totals = jnp.zeros((layers, D, D), jnp.float32)
    totals, _ = lax.scan(one_pipe, totals, (section_input, section_cotan, pipe_template))
    return totals
```

```python
import jax
import jax.numpy as jnp
from jax import lax
from jax.sharding import PartitionSpec as P

epsilon = 1e-05


def forward_rows(h_cols):
    gathered = lax.all_gather(h_cols, "tensor", axis=1, tiled=True)
    values = gathered.astype(jnp.float32)
    inv_rms = lax.rsqrt(jnp.mean(values * values, axis=1, keepdims=True) + epsilon)
    active = jax.nn.silu(values * inv_rms).astype(jnp.bfloat16)
    return (gathered, inv_rms, active)


def fetch_layer(weights, layer_ids, pipe_count, pipe_idx):
    if pipe_count == 2:
        own = lax.dynamic_index_in_dim(weights, layer_ids[pipe_idx], 0, keepdims=False)
        peer = lax.dynamic_index_in_dim(weights, layer_ids[1 - pipe_idx], 0, keepdims=False)
        other = lax.ppermute(peer, "pipe", [(0, 1), (1, 0)])
        return own, other
    block_rows = jnp.take(weights, layer_ids, axis=0, mode="clip")
    received = lax.all_to_all(block_rows, "pipe", split_axis=0, concat_axis=0, tiled=True)
    return (received.reshape(-1, received.shape[2]),)


def forward_product(active, parts, pipe_idx):
    if len(parts) == 1:
        return jnp.dot(active, parts[0], preferred_element_type=jnp.float32)
    rows = parts[0].shape[0]
    mine = lax.dynamic_slice_in_dim(active, pipe_idx * rows, rows, 1)
    rest = lax.dynamic_slice_in_dim(active, (1 - pipe_idx) * rows, rows, 1)
    return jnp.dot(mine, parts[0], preferred_element_type=jnp.float32) + jnp.dot(
        rest, parts[1], preferred_element_type=jnp.float32
    )


def backward_product(cotan, parts, pipe_idx):
    out = [
        jnp.einsum("tc,dc->td", cotan, part, preferred_element_type=jnp.float32).astype(
            jnp.bfloat16
        )
        for part in parts
    ]
    if len(out) == 1:
        return out[0]
    low = jnp.where(pipe_idx == 0, out[0], out[1])
    high = jnp.where(pipe_idx == 0, out[1], out[0])
    return jnp.concatenate([low, high], axis=1)


def norm_backward(summed, values, inv_rms):
    normed = values * inv_rms
    gate_sig = jax.nn.sigmoid(normed)
    return summed * gate_sig * (1.0 + normed * (1.0 - gate_sig))


def shards(section_input, section_cotan, weights, section_cuts, pipe_template):
    pipe_count = lax.axis_size("pipe")
    sections = lax.axis_size("section")
    layers = weights.shape[0]
    pipe_idx = lax.axis_index("pipe")
    section_idx = lax.axis_index("section")
    template_pick = (
        pipe_template[:, None] == jnp.arange(section_cuts.shape[0], dtype=jnp.int32)[None, :]
    ).astype(jnp.int32)
    starts = jnp.sum(template_pick[:, :, None] * section_cuts[None, :, :sections], axis=1)
    stops = jnp.sum(template_pick[:, :, None] * section_cuts[None, :, 1:], axis=1)
    section_pick = (jnp.arange(sections, dtype=jnp.int32) == section_idx).astype(jnp.int32)
    pipe_pick = (jnp.arange(pipe_count, dtype=jnp.int32) == pipe_idx).astype(jnp.float32)
    here_start = jnp.sum(starts * section_pick[None, :], axis=1)
    here_stop = jnp.sum(stops * section_pick[None, :], axis=1)
    second_ids = jnp.minimum(here_start + 1, layers - 1)
    second_flags = (here_start + 1 < here_stop).astype(jnp.float32)
    my_live = jnp.sum(second_flags * pipe_pick)
    first_parts = fetch_layer(weights, here_start, pipe_count, pipe_idx)
    second_parts = fetch_layer(weights, second_ids, pipe_count, pipe_idx)
    h_first = section_input[0, 0]
    gathered_first, inv_first, active_first = forward_rows(h_first)
    out_first = forward_product(active_first, first_parts, pipe_idx)
    h_second = (h_first.astype(jnp.float32) + out_first).astype(jnp.bfloat16)
    gathered_second, inv_second, active_second = forward_rows(h_second)
    cotan_low = section_cotan[0, 0]
    cotan = cotan_low.astype(jnp.float32)
    grad_second = (
        jnp.einsum("td,tc->dc", active_second, cotan_low, preferred_element_type=jnp.float32)
        * my_live
    )
    col_width = h_second.shape[1]
    partial_value = backward_product(cotan_low, second_parts, pipe_idx)
    summed = lax.psum_scatter(
        partial_value, "tensor", scatter_dimension=1, tiled=True
    ).astype(jnp.float32)
    values = h_second.astype(jnp.float32)
    d_norm = norm_backward(summed, values, inv_second)
    mean_term = lax.psum(jnp.sum(values * d_norm, axis=1), "tensor")[:, None] / (
        col_width * lax.axis_size("tensor")
    )
    d_rows = inv_second * d_norm - values * inv_second * inv_second * inv_second * mean_term
    cotan_first = cotan + my_live * d_rows
    grad_first = jnp.einsum(
        "td,tc->dc",
        active_first,
        cotan_first.astype(jnp.bfloat16),
        preferred_element_type=jnp.float32,
    )
    all_first = starts.reshape(-1)
    all_second = jnp.minimum(starts + 1, layers - 1).reshape(-1)
    pieces = []
    for layer_grad in (grad_first, grad_second):
        blocks = layer_grad.astype(jnp.bfloat16).reshape(
            pipe_count * sections, -1, layer_grad.shape[1]
        )
        pieces.append(
            lax.all_to_all(
                blocks, ("pipe", "section"), split_axis=0, concat_axis=0, tiled=True
            )
        )
    select = (
        jnp.arange(layers, dtype=jnp.int32)[:, None]
        == jnp.concatenate([all_first, all_second])[None, :]
    ).astype(jnp.bfloat16)
    count = all_first.shape[0]
    return jnp.einsum(
        "lq,qrc->lrc", select[:, :count], pieces[0], preferred_element_type=jnp.float32
    ) + jnp.einsum(
        "lq,qrc->lrc", select[:, count:], pieces[1], preferred_element_type=jnp.float32
    )


def solution(mesh):
    in_specs = (
        P("pipe", "section", None, "tensor"),
        P("pipe", "section", None, "tensor"),
        P(None, "pipe", "tensor"),
        P(),
        P(),
    )
    out_specs = P(None, ("pipe", "section"), "tensor")
    return jax.shard_map(shards, mesh=mesh, in_specs=in_specs, out_specs=out_specs, check_vma=False)
```
